256 devices in a mesh: qrow: 16 (over x, y_hi, core), kcol: 16 (over y_lo, z).
Axes of the slice: x: 4, y: 4 (y_hi: 2, y_lo: 2; y = y_hi * 2 + y_lo), z: 8, core: 2. Of those that a mesh axis runs over, the one named last changes fastest.
Arguments:
- query_states: bfloat16 [32768, 512], P(('qrow', 'kcol')), may hold values from -8 to 8
- key_states: bfloat16 [32768, 512], P(('kcol', 'qrow')), may hold values from -8 to 8
- value_states: bfloat16 [32768, 512], P(('kcol', 'qrow')), may hold values from -6 to 6
- saved_output: bfloat16 [32768, 512], P(('qrow', 'kcol')), may hold values from -0.59765625 to 0.59765625
- output_grad: bfloat16 [32768, 512], P(('qrow', 'kcol')), may hold values from -6 to 6
- normalizer: float32 [32768, 4], P(('qrow', 'kcol')), as said below
- doc_lengths: int32 [8], replicated, may hold values from 1 to 8192, as said below
Outputs:
- query_grad: bfloat16 [32768, 512], P(('qrow', 'kcol'))
- key_grad: bfloat16 [32768, 512], P(('kcol', 'qrow'))
- value_grad: bfloat16 [32768, 512], P(('kcol', 'qrow'))
The draws below stay inside these ranges and needn't reach their ends.
Inputs may be any that keep to these rules, and one draw needn't show every extreme that they name: `doc_lengths`: the 8 lengths sum to 32768; exactly one of them equals 8192, every other one is smaller. normalizer[p, h] is the logarithm of the sum of exp(scores[h, p, t]) over the t that allowed admits, computed in float32 from query_states, key_states and doc_lengths.
All inputs are finite; a program needn't handle non-finite values.
Results may differ from the reference program's by a relative error of at most 0.005.
Values may be sent and summed in bfloat16 or wider, within the bound.
No kernel may reach another device: no remote copies, remote signals or barrier semaphores. Data moves between devices by JAX's collectives and lax.ppermute only.
A program may use at most 192 MiB of HBM per device.

```python
import jax
import jax.numpy as jnp
from jax import lax

HEAD_DIM = 128
KV_HEADS = 4
GROUP = 1
TOK = 32768
DOCS = 8
MOST = 8192


def make_queries(key):
    sample = jnp.clip(jax.random.normal(jax.random.fold_in(key, 101), (TOK, KV_HEADS * GROUP * HEAD_DIM), jnp.float32), -4.0, 4.0)
    return sample.astype(jnp.bfloat16)


def make_keys(key):
    sample = jnp.clip(jax.random.normal(jax.random.fold_in(key, 201), (TOK, KV_HEADS * HEAD_DIM), jnp.float32), -4.0, 4.0)
    return sample.astype(jnp.bfloat16)


def make_lengths(key):
    weights = jax.random.randint(jax.random.fold_in(key, 301), (DOCS - 1,), 2, 4).astype(jnp.int32)
    remaining = TOK - MOST - (DOCS - 1)
    others = 1 + remaining * weights // jnp.sum(weights)
    leftover = TOK - MOST - jnp.sum(others)
    others = others + (jnp.arange(DOCS - 1, dtype=jnp.int32) < leftover).astype(jnp.int32)
    longest_at = jax.random.randint(jax.random.fold_in(key, 302), (), 0, DOCS).astype(jnp.int32)
    places = jnp.arange(DOCS, dtype=jnp.int32)
    source = jnp.clip(places - (places > longest_at).astype(jnp.int32), 0, DOCS - 2)
    return jnp.where(places == longest_at, MOST, others[source]).astype(jnp.int32)


def draw_query_states(key, part):
    return make_queries(key)


def draw_key_states(key, part):
    return make_keys(key)


def draw_doc_lengths(key, part):
    return make_lengths(key)


def draw_normalizer(key, part):
    scaling = HEAD_DIM ** (-0.5)
    queries = make_queries(key).astype(jnp.float32).reshape(TOK, KV_HEADS, GROUP, HEAD_DIM).transpose(1, 0, 2, 3)
    keys_all = make_keys(key).astype(jnp.float32).reshape(TOK, KV_HEADS, HEAD_DIM).transpose(1, 0, 2)
    lengths = make_lengths(key)
    positions = jnp.arange(TOK, dtype=jnp.int32)
    doc_ends = jnp.cumsum(lengths)
    documents = jnp.sum((positions[:, None] >= doc_ends[None, :]).astype(jnp.int32), axis=1)
    block_rows = 512 if TOK % 512 == 0 else TOK
    block_count = TOK // block_rows
    window = min(block_rows + MOST, TOK)

    def per_head(operands):
        query_head, key_head = operands

        def per_block(block_index):
            start_row = block_index * block_rows
            key_start = jnp.clip(start_row - MOST, 0, TOK - window).astype(jnp.int32)
            query_rows = lax.dynamic_slice_in_dim(query_head, start_row, block_rows, 0)
            key_rows = lax.dynamic_slice_in_dim(key_head, key_start, window, 0)
            key_pos = lax.dynamic_slice_in_dim(positions, key_start, window, 0)
            key_doc = lax.dynamic_slice_in_dim(documents, key_start, window, 0)
            query_pos = start_row + jnp.arange(block_rows, dtype=jnp.int32)
            query_doc = lax.dynamic_slice_in_dim(documents, start_row, block_rows, 0)
            allowed = (key_pos[None, :] <= query_pos[:, None]) & (key_doc[None, :] == query_doc[:, None])
            scores = jnp.einsum('qgd,kd->qgk', query_rows, key_rows) * scaling
            masked = jnp.where(allowed[:, None, :], scores, -1e+30)
            highest = jnp.max(masked, axis=2, keepdims=True)
            totals = jnp.sum(jnp.where(allowed[:, None, :], jnp.exp(masked - highest), 0.0), axis=2)
            return highest[:, :, 0] + jnp.log(totals)
        return lax.map(per_block, jnp.arange(block_count, dtype=jnp.int32)).reshape(TOK, GROUP)
    result = lax.map(per_head, (queries, keys_all))
    return result.transpose(1, 0, 2).reshape(TOK, KV_HEADS * GROUP).astype(jnp.float32)


def level_of(stream_key, shape, split, smallest, largest):
    def one(position, parts):
        draws = jax.random.uniform(jax.random.fold_in(jax.random.fold_in(stream_key, 6), position), (parts,), jnp.float32, smallest / len(split), largest / len(split))
        return jnp.repeat(jnp.exp(draws), shape[position] // parts).reshape((-1,) + (1,) * (len(shape) - position - 1))

    factor_of = one(*split[0])
    for cut in split[1:]:
        factor_of = factor_of * one(*cut)
    return factor_of


def gaussian(key, dims, deviation, most, shards=(), kind=jnp.bfloat16):
    loudness = level_of(key, dims, shards, -0.22, 0.18) if shards else 1.0
    array = jax.random.normal(key, dims, jnp.float32) * deviation * loudness
    return jnp.minimum(jnp.maximum(array, -most), most).astype(kind)


def setup_inputs(seed: int = 0) -> dict:
    arg_keys = jax.random.split(jax.random.key(seed), 8)
    query_states = draw_query_states(jax.random.fold_in(arg_keys[7], 71), 0)
    key_states = draw_key_states(jax.random.fold_in(arg_keys[7], 71), 0)
    value_states = gaussian(arg_keys[2], (TOK, KV_HEADS * HEAD_DIM), 1.0, 6.0, ((0, 256),))
    saved_output = gaussian(arg_keys[3], (TOK, KV_HEADS * GROUP * HEAD_DIM), 0.1, 0.59765625, ((0, 256),))
    output_grad = gaussian(arg_keys[4], (TOK, KV_HEADS * GROUP * HEAD_DIM), 1.0, 6.0, ((0, 256),))
    normalizer = draw_normalizer(jax.random.fold_in(arg_keys[7], 71), 0)
    doc_lengths = draw_doc_lengths(jax.random.fold_in(arg_keys[7], 71), 0)
    return {"query_states": query_states, "key_states": key_states, "value_states": value_states, "saved_output": saved_output, "output_grad": output_grad, "normalizer": normalizer, "doc_lengths": doc_lengths}


def document_ids(doc_lengths, positions):
    doc_ends = jnp.cumsum(doc_lengths)
    return jnp.sum((positions[:, None] >= doc_ends[None, :]).astype(jnp.int32), axis=1)


def reference(query_states, key_states, value_states, saved_output, output_grad, normalizer, doc_lengths):
    scaling = HEAD_DIM ** -0.5
    head_count = KV_HEADS * GROUP
    positions = jnp.arange(TOK, dtype=jnp.int32)
    documents = document_ids(doc_lengths, positions)
    row_delta = jnp.sum((output_grad.astype(jnp.float32) * saved_output.astype(jnp.float32)).reshape(TOK, head_count, HEAD_DIM), axis=2)
    block_rows = 512 if TOK % 512 == 0 else TOK
    block_count = TOK // block_rows
    window = min(block_rows + MOST, TOK)
    query_heads = query_states.astype(jnp.float32).reshape(TOK, KV_HEADS, GROUP, HEAD_DIM).transpose(1, 0, 2, 3)
    grad_heads = output_grad.astype(jnp.float32).reshape(TOK, KV_HEADS, GROUP, HEAD_DIM).transpose(1, 0, 2, 3)
    key_heads = key_states.astype(jnp.float32).reshape(TOK, KV_HEADS, HEAD_DIM).transpose(1, 0, 2)
    value_heads = value_states.astype(jnp.float32).reshape(TOK, KV_HEADS, HEAD_DIM).transpose(1, 0, 2)
    norm_heads = normalizer.reshape(TOK, KV_HEADS, GROUP).transpose(1, 0, 2)
    delta_heads = row_delta.reshape(TOK, KV_HEADS, GROUP).transpose(1, 0, 2)

    def one_head(operands):
        query_all, grad_all, key_all, value_all, norm_all, delta_all = operands

        def one_block(running, block_index):
            key_acc, value_acc = running
            start_row = block_index * block_rows
            key_start = jnp.clip(start_row - MOST, 0, TOK - window).astype(jnp.int32)
            query_rows = lax.dynamic_slice_in_dim(query_all, start_row, block_rows, 0)
            grad_rows = lax.dynamic_slice_in_dim(grad_all, start_row, block_rows, 0)
            norm_rows = lax.dynamic_slice_in_dim(norm_all, start_row, block_rows, 0)
            delta_rows = lax.dynamic_slice_in_dim(delta_all, start_row, block_rows, 0)
            key_rows = lax.dynamic_slice_in_dim(key_all, key_start, window, 0)
            value_rows = lax.dynamic_slice_in_dim(value_all, key_start, window, 0)
            key_pos = lax.dynamic_slice_in_dim(positions, key_start, window, 0)
            key_doc = lax.dynamic_slice_in_dim(documents, key_start, window, 0)
            query_pos = start_row + jnp.arange(block_rows, dtype=jnp.int32)
            query_doc = lax.dynamic_slice_in_dim(documents, start_row, block_rows, 0)
            allowed = (key_pos[None, :] <= query_pos[:, None]) & (key_doc[None, :] == query_doc[:, None])
            scores = jnp.einsum("qgd,kd->gqk", query_rows, key_rows) * scaling
            probability = jnp.where(allowed[None], jnp.exp(scores - norm_rows.T[:, :, None]), 0.0)
            prob_grad = jnp.einsum("qgd,kd->gqk", grad_rows, value_rows)
            score_grad = probability * (prob_grad - delta_rows.T[:, :, None])
            prob_half = lax.optimization_barrier(probability.astype(jnp.bfloat16)).astype(jnp.float32)
            grad_half = lax.optimization_barrier(score_grad.astype(jnp.bfloat16)).astype(jnp.float32)
            value_add = jnp.einsum("gqk,qgd->kd", prob_half, grad_rows)
            key_add = jnp.einsum("gqk,qgd->kd", grad_half, query_rows)
            value_acc = lax.dynamic_update_slice_in_dim(value_acc, lax.dynamic_slice_in_dim(value_acc, key_start, window, 0) + value_add, key_start, 0)
            key_acc = lax.dynamic_update_slice_in_dim(key_acc, lax.dynamic_slice_in_dim(key_acc, key_start, window, 0) + key_add, key_start, 0)
            query_part = jnp.einsum("gqk,kd->qgd", grad_half, key_rows) * scaling
            return (key_acc, value_acc), query_part

        empty_rows = jnp.zeros((TOK, HEAD_DIM), jnp.float32)
        (key_acc, value_acc), query_parts = lax.scan(one_block, (empty_rows, empty_rows), jnp.arange(block_count, dtype=jnp.int32))
        return query_parts.reshape(TOK, GROUP, HEAD_DIM), key_acc * scaling, value_acc

    query_all_grad, key_all_grad, value_all_grad = lax.map(one_head, (query_heads, grad_heads, key_heads, value_heads, norm_heads, delta_heads))
    query_grad = query_all_grad.transpose(1, 0, 2, 3).reshape(TOK, head_count * HEAD_DIM).astype(jnp.bfloat16)
    key_grad = key_all_grad.transpose(1, 0, 2).reshape(TOK, KV_HEADS * HEAD_DIM).astype(jnp.bfloat16)
    value_grad = value_all_grad.transpose(1, 0, 2).reshape(TOK, KV_HEADS * HEAD_DIM).astype(jnp.bfloat16)
    return (query_grad, key_grad, value_grad)
```

```python
import math

import jax
import jax.numpy as jnp
from jax import lax
from jax.experimental import pallas as pl
from jax.experimental.pallas import tpu as pltpu
from jax.sharding import PartitionSpec as P

HEAD_DIM = 128
HEADS = 4
BLOCK = 2048
CHUNK = 128
WAYS = 4
STRIP = CHUNK // WAYS
REACH = 5
KSPAN = 1024
KROWS = KSPAN // WAYS
QROWS = 512
SCALE = HEAD_DIM**-0.5
LOG2E = math.log2(math.e)
EXTRA = 16
OFF_DO = CHUNK
OFF_EXTRA = 2 * CHUNK
OFF_K = OFF_EXTRA + EXTRA
OFF_V = OFF_K + STRIP
PACKED = OFF_V + STRIP
F32 = jnp.float32
BF16 = jnp.bfloat16
VMEM = pl.BlockSpec(memory_space=pltpu.VMEM)
SMEM = pl.BlockSpec(memory_space=pltpu.SMEM)


def pieces(x):
    high = x.astype(BF16)
    rest = x - high.astype(F32)
    middle = rest.astype(BF16)
    low = (rest - middle.astype(F32)).astype(BF16)
    return [high, middle, low]


def pack_kernel(q_ref, k_ref, v_ref, o_ref, g_ref, n_ref, out_ref):
    rows = lax.broadcasted_iota(jnp.int32, (CHUNK, CHUNK), 0)
    cols = lax.broadcasted_iota(jnp.int32, (CHUNK, CHUNK), 1)
    eye = (rows == cols).astype(F32)
    norms = lax.dot_general(
        n_ref[...], eye, (((0,), (0,)), ((), ())),
        precision=lax.Precision.HIGHEST, preferred_element_type=F32,
    ) * LOG2E
    ones = jnp.ones((8, HEAD_DIM), F32)
    for h in range(HEADS):
        at = slice(h * HEAD_DIM, (h + 1) * HEAD_DIM)
        q, g = q_ref[:, at], g_ref[:, at]
        delta = lax.dot_general(
            ones, g.astype(F32) * o_ref[:, at].astype(F32), (((1,), (1,)), ((), ())),
            precision=lax.Precision.HIGHEST, preferred_element_type=F32,
        )[:1]
        extra = jnp.concatenate(
            [p.astype(F32) for p in pieces(norms[h : h + 1]) + pieces(delta)]
            + [jnp.zeros((EXTRA - 6, CHUNK), F32)], axis=0
        ).astype(BF16)
        for d in range(WAYS):
            t = h * WAYS + d
            out_ref[t, 0:CHUNK] = q
            out_ref[t, OFF_DO : OFF_DO + CHUNK] = g
            out_ref[t, OFF_EXTRA : OFF_EXTRA + EXTRA] = extra
            out_ref[t, OFF_K : OFF_K + STRIP] = k_ref[d * STRIP : (d + 1) * STRIP, at]
            out_ref[t, OFF_V : OFF_V + STRIP] = v_ref[d * STRIP : (d + 1) * STRIP, at]


def spread_kernel(in_ref, out_ref):
    count = out_ref.shape[0]
    for b in range(count):
        for back in range(REACH):
            out_ref[b, back] = in_ref[max(b - back, 0), OFF_K:PACKED]


def tiles_kernel(place_ref, lengths_ref, in_ref, kv_ref, dq_ref, dkv_ref, dk_acc, dv_acc, dq_acc):
    block = place_ref[0]
    strip = place_ref[1]
    ends = []
    total = jnp.int32(0)
    for e in range(lengths_ref.shape[0]):
        total = total + lengths_ref[e]
        ends.append(total)
    base = (block - (REACH - 1)) * BLOCK
    dk_acc[...] = jnp.zeros_like(dk_acc)
    dv_acc[...] = jnp.zeros_like(dv_acc)
    m_tile = QROWS // CHUNK
    j_tile = KROWS // STRIP
    per_block = BLOCK // KSPAN
    k_iota = lax.broadcasted_iota(jnp.int32, (KROWS, 1), 0)
    k_iota = (k_iota // STRIP) * CHUNK + k_iota % STRIP + strip * STRIP

    def query_tile(t, carry):
        first = block * BLOCK + t * QROWS
        doc_first = jnp.int32(0)
        q_pos = first + lax.broadcasted_iota(jnp.int32, (1, QROWS), 1)
        q_doc = jnp.zeros((1, QROWS), jnp.int32)
        for end in ends:
            doc_first = jnp.where(end <= first, end, doc_first)
            q_doc = jnp.where(end <= q_pos, end, q_doc)
        low = (doc_first - base) // KSPAN
        high = (first + QROWS - 1 - base) // KSPAN
        q = in_ref[pl.ds(t * m_tile, m_tile), 0:CHUNK].reshape(QROWS, HEAD_DIM)
        g = in_ref[pl.ds(t * m_tile, m_tile), OFF_DO : OFF_DO + CHUNK].reshape(QROWS, HEAD_DIM)
        extra = in_ref[pl.ds(t * m_tile, m_tile), OFF_EXTRA : OFF_EXTRA + EXTRA].astype(F32)

        def row(at):
            parts = [
                extra[m, at : at + 1] + extra[m, at + 1 : at + 2] + extra[m, at + 2 : at + 3]
                for m in range(m_tile)
            ]
            return jnp.concatenate(parts, axis=1)

        norm, delta = row(0), row(3)
        dq_acc[...] = jnp.zeros_like(dq_acc)

        def key_tile(kt, carry):
            js = pl.ds((kt % per_block) * j_tile, j_tile)
            back = REACH - 1 - kt // per_block
            k = kv_ref[js, back, 0:STRIP].reshape(KROWS, HEAD_DIM)
            v = kv_ref[js, back, STRIP : 2 * STRIP].reshape(KROWS, HEAD_DIM)
            k_pos = k_iota + (base + kt * KSPAN)
            across = (((1,), (1,)), ((), ()))
            s = lax.dot_general(k, q, across, preferred_element_type=F32)
            p = jnp.exp2(s * (SCALE * LOG2E) - norm)
            p = jnp.where((k_pos <= q_pos) & (k_pos >= q_doc), p, 0.0)
            dp = lax.dot_general(v, g, across, preferred_element_type=F32)
            ds = (p * (dp - delta)).astype(BF16)
            p = p.astype(BF16)
            dv_acc[kt] += jnp.dot(p, g, preferred_element_type=F32)
            dk_acc[kt] += jnp.dot(ds, q, preferred_element_type=F32)
            dq_acc[...] += lax.dot_general(
                ds, k, (((0,), (0,)), ((), ())), preferred_element_type=F32
            )
            return carry

        lax.fori_loop(low, high + 1, key_tile, 0)
        dq_ref[pl.ds(t * m_tile, m_tile)] = (
            (dq_acc[...] * SCALE).astype(BF16).reshape(m_tile, CHUNK, HEAD_DIM)
        )
        return carry

    lax.fori_loop(0, BLOCK // QROWS, query_tile, 0)
    for kt in range(REACH * per_block):
        js = slice((kt % per_block) * j_tile, (kt % per_block + 1) * j_tile)
        back = REACH - 1 - kt // per_block
        dkv_ref[js, back, 0:STRIP] = (dk_acc[kt] * SCALE).astype(BF16).reshape(j_tile, STRIP, HEAD_DIM)
        dkv_ref[js, back, STRIP : 2 * STRIP] = dv_acc[kt].astype(BF16).reshape(j_tile, STRIP, HEAD_DIM)


def collect_kernel(dq_ref, dkv_ref, out_ref):
    count = out_ref.shape[0]
    for b in range(count):
        out_ref[b, 0:CHUNK] = dq_ref[b]
        total = dkv_ref[b, 0].astype(F32)
        for back in range(1, REACH):
            if b + back < count:
                total = total + dkv_ref[b + back, back].astype(F32)
        out_ref[b, CHUNK : CHUNK + 2 * STRIP] = total.astype(BF16)


def unpack_kernel(in_ref, dq_ref, dk_ref, dv_ref):
    for h in range(HEADS):
        at = slice(h * HEAD_DIM, (h + 1) * HEAD_DIM)
        total = in_ref[h * WAYS, 0:CHUNK].astype(F32)
        for d in range(1, WAYS):
            total = total + in_ref[h * WAYS + d, 0:CHUNK].astype(F32)
        dq_ref[:, at] = total.astype(BF16)
        for d in range(WAYS):
            rows = slice(d * STRIP, (d + 1) * STRIP)
            dk_ref[rows, at] = in_ref[h * WAYS + d, CHUNK : CHUNK + STRIP]
            dv_ref[rows, at] = in_ref[h * WAYS + d, CHUNK + STRIP : CHUNK + 2 * STRIP]


def shape(*dims, dtype=BF16):
    return jax.ShapeDtypeStruct(dims, dtype)


def per_device(query_states, key_states, value_states, saved_output, output_grad, normalizer, doc_lengths):
    blocks = lax.axis_size("qrow")
    ways = lax.axis_size("kcol")
    place = jnp.stack([lax.axis_index("qrow"), lax.axis_index("kcol") % WAYS]).astype(jnp.int32)
    packed = pl.pallas_call(
        pack_kernel,
        in_specs=[VMEM] * 6,
        out_specs=VMEM,
        out_shape=shape(ways, PACKED, HEAD_DIM),
    )(query_states, key_states, value_states, saved_output, output_grad, normalizer)
    mine = lax.all_to_all(packed, "kcol", 0, 0)
    spread = pl.pallas_call(
        spread_kernel,
        in_specs=[VMEM],
        out_specs=VMEM,
        out_shape=shape(blocks, REACH, 2 * STRIP, HEAD_DIM),
    )(mine)
    keys = lax.all_to_all(spread, "qrow", 0, 0)
    tiles = REACH * BLOCK // KSPAN
    dq_part, dkv_part = pl.pallas_call(
        tiles_kernel,
        in_specs=[SMEM, SMEM, VMEM, VMEM],
        out_specs=[VMEM, VMEM],
        out_shape=[shape(ways, CHUNK, HEAD_DIM), shape(blocks, REACH, 2 * STRIP, HEAD_DIM)],
        scratch_shapes=[
            pltpu.VMEM((tiles, KROWS, HEAD_DIM), F32),
            pltpu.VMEM((tiles, KROWS, HEAD_DIM), F32),
            pltpu.VMEM((QROWS, HEAD_DIM), F32),
        ],
        compiler_params=pltpu.CompilerParams(vmem_limit_bytes=40 * 1024 * 1024),
    )(place, doc_lengths, mine, keys)
    dkv = lax.all_to_all(dkv_part, "qrow", 0, 0)
    sums = pl.pallas_call(
        collect_kernel,
        in_specs=[VMEM, VMEM],
        out_specs=VMEM,
        out_shape=shape(ways, CHUNK + 2 * STRIP, HEAD_DIM),
    )(dq_part, dkv)
    back = lax.all_to_all(sums, "kcol", 0, 0)
    width = HEADS * HEAD_DIM
    return tuple(
        pl.pallas_call(
            unpack_kernel,
            in_specs=[VMEM],
            out_specs=[VMEM] * 3,
            out_shape=[shape(CHUNK, width)] * 3,
        )(back)
    )


def solution(mesh):
    rows = P(("qrow", "kcol"), None)
    keys = P(("kcol", "qrow"), None)
    return jax.shard_map(
        per_device,
        mesh=mesh,
        in_specs=(rows, keys, keys, rows, rows, rows, P()),
        out_specs=(rows, keys, keys),
        check_vma=False,
    )
```

```python
import math

import jax
import jax.numpy as jnp
from jax import lax
from jax.experimental import pallas as pl
from jax.experimental.pallas import tpu as pltpu
from jax.sharding import Mesh
from jax.sharding import PartitionSpec as P

HEAD_DIM = 128
HEADS = 4
BLOCK = 2048
CHUNK = 128
WAYS = 4
STRIP = CHUNK // WAYS
REACH = 5
KSPAN = 1024
KROWS = KSPAN // WAYS
QROWS = 1024
SCALE = HEAD_DIM**-0.5
LOG2E = math.log2(math.e)
EXTRA = 16
OFF_DO = STRIP
OFF_K = 2 * STRIP
OFF_V = 3 * STRIP
OFF_EXTRA = 4 * STRIP
PACKED = OFF_EXTRA + EXTRA
KCOL = ("kcol_h", "kcol_s")
STRIPS = "kcol_s"
F32 = jnp.float32
BF16 = jnp.bfloat16
VMEM = pl.BlockSpec(memory_space=pltpu.VMEM)
SMEM = pl.BlockSpec(memory_space=pltpu.SMEM)


def pieces(x):
    high = x.astype(BF16)
    rest = x - high.astype(F32)
    middle = rest.astype(BF16)
    low = (rest - middle.astype(F32)).astype(BF16)
    return [high, middle, low]


def head_and_strip(t):
    return t // WAYS, t % WAYS


def pack_kernel(q_ref, k_ref, v_ref, o_ref, g_ref, n_ref, out_ref):
    norms = n_ref[...] * LOG2E
    ones = jnp.ones((8, HEAD_DIM), F32)
    extras = []
    for h in range(HEADS):
        at = slice(h * HEAD_DIM, (h + 1) * HEAD_DIM)
        delta = lax.dot_general(
            ones, g_ref[:, at].astype(F32) * o_ref[:, at].astype(F32), (((1,), (1,)), ((), ())),
            precision=lax.Precision.HIGHEST, preferred_element_type=F32,
        )[:1]
        extras.append(
            jnp.concatenate(
                [p.astype(F32) for p in pieces(norms[h : h + 1]) + pieces(delta)]
                + [jnp.zeros((EXTRA - 6, CHUNK), F32)], axis=0
            ).astype(BF16)
        )
    for t in range(out_ref.shape[0]):
        h, d = head_and_strip(t)
        at = slice(h * HEAD_DIM, (h + 1) * HEAD_DIM)
        rows = slice(d * STRIP, (d + 1) * STRIP)
        out_ref[t, 0:STRIP] = q_ref[rows, at]
        out_ref[t, OFF_DO : OFF_DO + STRIP] = g_ref[rows, at]
        out_ref[t, OFF_K : OFF_K + STRIP] = k_ref[rows, at]
        out_ref[t, OFF_V : OFF_V + STRIP] = v_ref[rows, at]
        out_ref[t, OFF_EXTRA:PACKED] = extras[h]


def spread_kernel(in_ref, out_ref, qg_ref):
    count = out_ref.shape[0]
    qg_ref[...] = in_ref[:, 0 : 2 * STRIP]
    for b in range(count):
        for back in range(REACH):
            out_ref[b, back] = in_ref[max(b - back, 0), OFF_K : OFF_K + 2 * STRIP]


def tiles_kernel(
    place_ref, lengths_ref, in_ref, qg0, qg1, qg2, qg3, kv_ref,
    dq0, dq1, dq2, dq3, dkv_ref, dk_acc, dv_acc, dq_acc, q_all, g_all, dq_all,
):
    block = place_ref[0]
    strip = place_ref[1]
    ends = []
    total = jnp.int32(0)
    for e in range(lengths_ref.shape[0]):
        total = total + lengths_ref[e]
        ends.append(total)
    base = (block - (REACH - 1)) * BLOCK
    for s, ref in enumerate((qg0, qg1, qg2, qg3)):
        q_all[:, strip ^ s] = ref[:, 0:STRIP]
        g_all[:, strip ^ s] = ref[:, STRIP : 2 * STRIP]
    dk_acc[...] = jnp.zeros_like(dk_acc)
    dv_acc[...] = jnp.zeros_like(dv_acc)
    m_tile = QROWS // CHUNK
    j_tile = KROWS // STRIP
    per_block = BLOCK // KSPAN
    k_iota = lax.broadcasted_iota(jnp.int32, (KROWS, 1), 0)
    k_iota = (k_iota // STRIP) * CHUNK + k_iota % STRIP + strip * STRIP

    def query_tile(t, carry):
        first = block * BLOCK + t * QROWS
        last = first + QROWS - 1
        doc_first = jnp.int32(0)
        doc_last = jnp.int32(0)
        q_pos = first + lax.broadcasted_iota(jnp.int32, (1, QROWS), 1)
        q_doc = jnp.zeros((1, QROWS), jnp.int32)
        for end in ends:
            doc_first = jnp.where(end <= first, end, doc_first)
            doc_last = jnp.where(end <= last, end, doc_last)
            q_doc = jnp.where(end <= q_pos, end, q_doc)
        low = (doc_first - base) // KSPAN
        high = (last - base) // KSPAN
        q = q_all[pl.ds(t * m_tile, m_tile)].reshape(QROWS, HEAD_DIM)
        g = g_all[pl.ds(t * m_tile, m_tile)].reshape(QROWS, HEAD_DIM)
        extra = in_ref[pl.ds(t * m_tile, m_tile), OFF_EXTRA:PACKED].astype(F32)

        def row(at):
            parts = [
                extra[m, at : at + 1] + extra[m, at + 1 : at + 2] + extra[m, at + 2 : at + 3]
                for m in range(m_tile)
            ]
            return jnp.concatenate(parts, axis=1)

        norm, delta = row(0), row(3)
        dq_acc[...] = jnp.zeros_like(dq_acc)

        def one_tile(kt, masked):
            js = pl.ds((kt % per_block) * j_tile, j_tile)
            back = REACH - 1 - kt // per_block
            k = kv_ref[js, back, 0:STRIP].reshape(KROWS, HEAD_DIM)
            v = kv_ref[js, back, STRIP : 2 * STRIP].reshape(KROWS, HEAD_DIM)
            across = (((1,), (1,)), ((), ()))
            s = lax.dot_general(k, q, across, preferred_element_type=F32)
            p = jnp.exp2(s * (SCALE * LOG2E) - norm)
            if masked:
                k_pos = k_iota + (base + kt * KSPAN)
                p = jnp.where((k_pos <= q_pos) & (k_pos >= q_doc), p, 0.0)
            dp = lax.dot_general(v, g, across, preferred_element_type=F32)
            ds = (p * (dp - delta)).astype(BF16)
            p = p.astype(BF16)
            dv_acc[kt] += jnp.dot(p, g, preferred_element_type=F32)
            dk_acc[kt] += jnp.dot(ds, q, preferred_element_type=F32)
            dq_acc[...] += lax.dot_general(
                k, ds, (((0,), (0,)), ((), ())), preferred_element_type=F32
            )

        def key_tile(kt, carry):
            start = base + kt * KSPAN
            whole = (start + KSPAN - 1 <= first) & (start >= doc_last)

            @pl.when(whole)
            def _():
                one_tile(kt, False)

            @pl.when(jnp.logical_not(whole))
            def _():
                one_tile(kt, True)

            return carry

        lax.fori_loop(low, high + 1, key_tile, 0)
        dq_all[pl.ds(t * m_tile, m_tile)] = (
            (dq_acc[...].T * SCALE).astype(BF16).reshape(m_tile, WAYS, STRIP, HEAD_DIM)
        )
        return carry

    lax.fori_loop(0, BLOCK // QROWS, query_tile, 0)
    for s, ref in enumerate((dq0, dq1, dq2, dq3)):
        ref[...] = dq_all[:, strip ^ s]
    for kt in range(REACH * per_block):
        js = slice((kt % per_block) * j_tile, (kt % per_block + 1) * j_tile)
        back = REACH - 1 - kt // per_block
        dkv_ref[js, back, 0:STRIP] = (dk_acc[kt] * SCALE).astype(BF16).reshape(j_tile, STRIP, HEAD_DIM)
        dkv_ref[js, back, STRIP : 2 * STRIP] = dv_acc[kt].astype(BF16).reshape(j_tile, STRIP, HEAD_DIM)


def collect_kernel(dq0, dq1, dq2, dq3, dkv_ref, out_ref):
    count = out_ref.shape[0]
    dq = dq0[...].astype(F32)
    for ref in (dq1, dq2, dq3):
        dq = dq + ref[...].astype(F32)
    out_ref[:, 0:STRIP] = dq.astype(BF16)
    for b in range(count):
        total = dkv_ref[b, 0].astype(F32)
        for back in range(1, REACH):
            if b + back < count:
                total = total + dkv_ref[b + back, back].astype(F32)
        out_ref[b, STRIP : 3 * STRIP] = total.astype(BF16)


def unpack_kernel(in_ref, dq_ref, dk_ref, dv_ref):
    for t in range(in_ref.shape[0]):
        h, d = head_and_strip(t)
        at = slice(h * HEAD_DIM, (h + 1) * HEAD_DIM)
        rows = slice(d * STRIP, (d + 1) * STRIP)
        dq_ref[rows, at] = in_ref[t, 0:STRIP]
        dk_ref[rows, at] = in_ref[t, STRIP : 2 * STRIP]
        dv_ref[rows, at] = in_ref[t, 2 * STRIP : 3 * STRIP]


def shape(*dims, dtype=BF16):
    return jax.ShapeDtypeStruct(dims, dtype)


def from_partner(x, s):
    return lax.ppermute(x, STRIPS, [(d, d ^ s) for d in range(WAYS)])


def call_tiles(place, doc_lengths, mine, qg, *rest):
    keys = rest[-1]
    ways, blocks = mine.shape[0], keys.shape[0]
    tiles = REACH * BLOCK // KSPAN
    return pl.pallas_call(
        tiles_kernel,
        in_specs=[SMEM, SMEM] + [VMEM] * 6,
        out_specs=[VMEM] * 5,
        out_shape=[shape(ways, STRIP, HEAD_DIM)] * 4 + [shape(blocks, REACH, 2 * STRIP, HEAD_DIM)],
        scratch_shapes=[
            pltpu.VMEM((tiles, KROWS, HEAD_DIM), F32),
            pltpu.VMEM((tiles, KROWS, HEAD_DIM), F32),
            pltpu.VMEM((HEAD_DIM, QROWS), F32),
        ] + [pltpu.VMEM((ways, WAYS, STRIP, HEAD_DIM), BF16)] * 3,
        compiler_params=pltpu.CompilerParams(vmem_limit_bytes=40 * 1024 * 1024),
    )(place, doc_lengths, mine, qg, *rest)


def per_device(query_states, key_states, value_states, saved_output, output_grad, normalizer, doc_lengths):
    blocks = lax.axis_size("qrow")
    ways = lax.axis_size(KCOL)
    place = jnp.stack([lax.axis_index("qrow"), lax.axis_index(STRIPS)]).astype(jnp.int32)
    packed = pl.pallas_call(
        pack_kernel,
        in_specs=[VMEM] * 6,
        out_specs=VMEM,
        out_shape=shape(ways, PACKED, HEAD_DIM),
    )(query_states, key_states, value_states, saved_output, output_grad, normalizer.T)
    mine = lax.all_to_all(packed, KCOL, 0, 0)
    spread, qg = pl.pallas_call(
        spread_kernel,
        in_specs=[VMEM],
        out_specs=[VMEM] * 2,
        out_shape=[shape(blocks, REACH, 2 * STRIP, HEAD_DIM), shape(ways, 2 * STRIP, HEAD_DIM)],
    )(mine)
    keys = lax.all_to_all(spread, "qrow", 0, 0)
    far = from_partner(qg, 2)
    others = [from_partner(qg, 1), far, from_partner(far, 1)]
    *dq_parts, dkv_part = call_tiles(place, doc_lengths, mine, qg, *others, keys)
    dkv = lax.all_to_all(dkv_part, "qrow", 0, 0)
    dq_parts = [dq_parts[0]] + [from_partner(dq_parts[s], s) for s in range(1, WAYS)]
    sums = pl.pallas_call(
        collect_kernel,
        in_specs=[VMEM] * 5,
        out_specs=VMEM,
        out_shape=shape(ways, 3 * STRIP, HEAD_DIM),
    )(*dq_parts, dkv)
    back = lax.all_to_all(sums, KCOL, 0, 0)
    width = HEADS * HEAD_DIM
    return tuple(
        pl.pallas_call(
            unpack_kernel,
            in_specs=[VMEM],
            out_specs=[VMEM] * 3,
            out_shape=[shape(CHUNK, width)] * 3,
        )(back)
    )


def solution(mesh):
    finer = Mesh(mesh.devices.reshape(mesh.shape["qrow"], HEADS, WAYS), ("qrow",) + KCOL)
    rows = P(("qrow",) + KCOL, None)
    keys = P(KCOL + ("qrow",), None)
    return jax.shard_map(
        per_device,
        mesh=finer,
        in_specs=(rows, keys, keys, rows, rows, rows, P()),
        out_specs=(rows, keys, keys),
        check_vma=False,
    )
```

```python
import math

import jax
import jax.numpy as jnp
from jax import lax
from jax.experimental import pallas as pl
from jax.experimental.pallas import tpu as pltpu
from jax.sharding import Mesh
from jax.sharding import PartitionSpec as P

HEAD_DIM = 128
HEADS = 4
BLOCK = 2048
CHUNK = 128
WAYS = 4
STRIP = CHUNK // WAYS
REACH = 5
KSPAN = 1024
KROWS = KSPAN // WAYS
QROWS = 1024
SCALE = HEAD_DIM**-0.5
LOG2E = math.log2(math.e)
EXTRA = 8
OFF_DO = STRIP
OFF_K = 2 * STRIP
OFF_V = 3 * STRIP
OFF_EXTRA = 4 * STRIP
PACKED = OFF_EXTRA + EXTRA
KCOL = ("kcol_h", "kcol_s")
STRIPS = "kcol_s"
F32 = jnp.float32
BF16 = jnp.bfloat16
VMEM = pl.BlockSpec(memory_space=pltpu.VMEM)
SMALL = pltpu.CompilerParams(vmem_limit_bytes=8 * 1024 * 1024)
SMEM = pl.BlockSpec(memory_space=pltpu.SMEM)


def pieces(x):
    high = x.astype(BF16)
    rest = x - high.astype(F32)
    middle = rest.astype(BF16)
    low = (rest - middle.astype(F32)).astype(BF16)
    return [high, middle, low]


def head_and_strip(t):
    return t // WAYS, t % WAYS


def pack_kernel(q_ref, k_ref, v_ref, o_ref, g_ref, n_ref, out_ref):
    norms = n_ref[...] * LOG2E
    ones = jnp.ones((8, HEAD_DIM), F32)
    extras = []
    for h in range(HEADS):
        at = slice(h * HEAD_DIM, (h + 1) * HEAD_DIM)
        delta = lax.dot_general(
            ones, g_ref[:, at].astype(F32) * o_ref[:, at].astype(F32), (((1,), (1,)), ((), ())),
            precision=lax.Precision.HIGHEST, preferred_element_type=F32,
        )[:1]
        extras.append(
            jnp.concatenate(
                [p.astype(F32) for p in pieces(norms[h : h + 1]) + pieces(delta)]
                + [jnp.zeros((EXTRA - 6, CHUNK), F32)], axis=0
            ).astype(BF16)
        )
    for t in range(out_ref.shape[0]):
        h, d = head_and_strip(t)
        at = slice(h * HEAD_DIM, (h + 1) * HEAD_DIM)
        rows = slice(d * STRIP, (d + 1) * STRIP)
        out_ref[t, 0:STRIP] = q_ref[rows, at]
        out_ref[t, OFF_DO : OFF_DO + STRIP] = g_ref[rows, at]
        out_ref[t, OFF_K : OFF_K + STRIP] = k_ref[rows, at]
        out_ref[t, OFF_V : OFF_V + STRIP] = v_ref[rows, at]
        out_ref[t, OFF_EXTRA:PACKED] = extras[h]


def spread_kernel(in_ref, out_ref, qg_ref):
    count = out_ref.shape[0]
    qg_ref[...] = in_ref[:, 0 : 2 * STRIP]
    for b in range(count):
        for back in range(REACH):
            out_ref[b, back] = in_ref[max(b - back, 0), OFF_K : OFF_K + 2 * STRIP]


def tiles_kernel(
    place_ref, lengths_ref, in_ref, qg0, qg1, qg2, qg3, kv_ref,
    dq0, dq1, dq2, dq3, dkv_ref, dk_acc, dv_acc, dq_acc, q_all, g_all, dq_all,
):
    block = place_ref[0]
    strip = place_ref[1]
    ends = []
    total = jnp.int32(0)
    for e in range(lengths_ref.shape[0]):
        total = total + lengths_ref[e]
        ends.append(total)
    base = (block - (REACH - 1)) * BLOCK
    for s, ref in enumerate((qg0, qg1, qg2, qg3)):
        q_all[:, strip ^ s] = ref[:, 0:STRIP]
        g_all[:, strip ^ s] = ref[:, STRIP : 2 * STRIP]
    dk_acc[...] = jnp.zeros_like(dk_acc)
    dv_acc[...] = jnp.zeros_like(dv_acc)
    m_tile = QROWS // CHUNK
    j_tile = KROWS // STRIP
    per_block = BLOCK // KSPAN
    k_iota = lax.broadcasted_iota(jnp.int32, (KROWS, 1), 0)
    k_iota = (k_iota // STRIP) * CHUNK + k_iota % STRIP + strip * STRIP

    def query_tile(t, carry):
        first = block * BLOCK + t * QROWS
        last = first + QROWS - 1
        doc_first = jnp.int32(0)
        doc_last = jnp.int32(0)
        q_pos = first + lax.broadcasted_iota(jnp.int32, (1, QROWS), 1)
        q_doc = jnp.zeros((1, QROWS), jnp.int32)
        for end in ends:
            doc_first = jnp.where(end <= first, end, doc_first)
            doc_last = jnp.where(end <= last, end, doc_last)
            q_doc = jnp.where(end <= q_pos, end, q_doc)
        low = (doc_first - base) // KSPAN
        high = (last - base) // KSPAN
        q = q_all[pl.ds(t * m_tile, m_tile)].reshape(QROWS, HEAD_DIM)
        g = g_all[pl.ds(t * m_tile, m_tile)].reshape(QROWS, HEAD_DIM)
        extra = in_ref[pl.ds(t * m_tile, m_tile), OFF_EXTRA:PACKED].astype(F32)

        def row(at):
            parts = [
                extra[m, at : at + 1] + extra[m, at + 1 : at + 2] + extra[m, at + 2 : at + 3]
                for m in range(m_tile)
            ]
            return jnp.concatenate(parts, axis=1)

        norm, delta = row(0), row(3)
        dq_acc[...] = jnp.zeros_like(dq_acc)

        def one_tile(kt, masked):
            js = pl.ds((kt % per_block) * j_tile, j_tile)
            back = REACH - 1 - kt // per_block
            k = kv_ref[js, back, 0:STRIP].reshape(KROWS, HEAD_DIM)
            v = kv_ref[js, back, STRIP : 2 * STRIP].reshape(KROWS, HEAD_DIM)
            across = (((1,), (1,)), ((), ()))
            s = lax.dot_general(k, q, across, preferred_element_type=F32)
            p = jnp.exp2(s * (SCALE * LOG2E) - norm)
            if masked:
                k_pos = k_iota + (base + kt * KSPAN)
                p = jnp.where((k_pos <= q_pos) & (k_pos >= q_doc), p, 0.0)
            dp = lax.dot_general(v, g, across, preferred_element_type=F32)
            ds = (p * (dp - delta)).astype(BF16)
            p = p.astype(BF16)
            dv_acc[kt] += jnp.dot(p, g, preferred_element_type=F32)
            dk_acc[kt] += jnp.dot(ds, q, preferred_element_type=F32)
            dq_acc[...] += lax.dot_general(
                k, ds, (((0,), (0,)), ((), ())), preferred_element_type=F32
            )

        def key_tile(kt, carry):
            start = base + kt * KSPAN
            whole = (start + KSPAN - 1 <= first) & (start >= doc_last)

            @pl.when(whole)
            def _():
                one_tile(kt, False)

            @pl.when(jnp.logical_not(whole))
            def _():
                one_tile(kt, True)

            return carry

        lax.fori_loop(low, high + 1, key_tile, 0)
        dq_all[pl.ds(t * m_tile, m_tile)] = (
            (dq_acc[...].T * SCALE).astype(BF16).reshape(m_tile, WAYS, STRIP, HEAD_DIM)
        )
        return carry

    lax.fori_loop(0, BLOCK // QROWS, query_tile, 0)
    for s, ref in enumerate((dq0, dq1, dq2, dq3)):
        ref[...] = dq_all[:, strip ^ s]
    for kt in range(REACH * per_block):
        js = slice((kt % per_block) * j_tile, (kt % per_block + 1) * j_tile)
        back = REACH - 1 - kt // per_block
        dkv_ref[js, back, 0:STRIP] = (dk_acc[kt] * SCALE).astype(BF16).reshape(j_tile, STRIP, HEAD_DIM)
        dkv_ref[js, back, STRIP : 2 * STRIP] = dv_acc[kt].astype(BF16).reshape(j_tile, STRIP, HEAD_DIM)


def collect_kernel(dq0, dq1, dq2, dq3, dkv_ref, out_ref):
    count = out_ref.shape[0]
    dq = dq0[...].astype(F32)
    for ref in (dq1, dq2, dq3):
        dq = dq + ref[...].astype(F32)
    out_ref[:, 0:STRIP] = dq.astype(BF16)
    for b in range(count):
        total = dkv_ref[b, 0].astype(F32)
        for back in range(1, REACH):
            if b + back < count:
                total = total + dkv_ref[b + back, back].astype(F32)
        out_ref[b, STRIP : 3 * STRIP] = total.astype(BF16)


def unpack_kernel(in_ref, dq_ref, dk_ref, dv_ref):
    for t in range(in_ref.shape[0]):
        h, d = head_and_strip(t)
        at = slice(h * HEAD_DIM, (h + 1) * HEAD_DIM)
        rows = slice(d * STRIP, (d + 1) * STRIP)
        dq_ref[rows, at] = in_ref[t, 0:STRIP]
        dk_ref[rows, at] = in_ref[t, STRIP : 2 * STRIP]
        dv_ref[rows, at] = in_ref[t, 2 * STRIP : 3 * STRIP]


def shape(*dims, dtype=BF16):
    return jax.ShapeDtypeStruct(dims, dtype)


def from_partner(x, s):
    return lax.ppermute(x, STRIPS, [(d, d ^ s) for d in range(WAYS)])


def call_tiles(place, doc_lengths, mine, qg, *rest):
    keys = rest[-1]
    ways, blocks = mine.shape[0], keys.shape[0]
    tiles = REACH * BLOCK // KSPAN
    return pl.pallas_call(
        tiles_kernel,
        in_specs=[SMEM, SMEM] + [VMEM] * 6,
        out_specs=[VMEM] * 5,
        out_shape=[shape(ways, STRIP, HEAD_DIM)] * 4 + [shape(blocks, REACH, 2 * STRIP, HEAD_DIM)],
        scratch_shapes=[
            pltpu.VMEM((tiles, KROWS, HEAD_DIM), F32),
            pltpu.VMEM((tiles, KROWS, HEAD_DIM), F32),
            pltpu.VMEM((HEAD_DIM, QROWS), F32),
        ] + [pltpu.VMEM((ways, WAYS, STRIP, HEAD_DIM), BF16)] * 3,
        compiler_params=pltpu.CompilerParams(vmem_limit_bytes=24 * 1024 * 1024),
    )(place, doc_lengths, mine, qg, *rest)


def per_device(query_states, key_states, value_states, saved_output, output_grad, normalizer, doc_lengths):
    blocks = lax.axis_size("qrow")
    ways = lax.axis_size(KCOL)
    place = jnp.stack([lax.axis_index("qrow"), lax.axis_index(STRIPS)]).astype(jnp.int32)
    packed = pl.pallas_call(
        pack_kernel,
        compiler_params=pltpu.CompilerParams(vmem_limit_bytes=60 * 1024 * 1024),
        in_specs=[VMEM] * 6,
        out_specs=VMEM,
        out_shape=shape(ways, PACKED, HEAD_DIM),
    )(query_states, key_states, value_states, saved_output, output_grad, normalizer.T)
    mine = lax.all_to_all(packed, KCOL, 0, 0)
    spread, qg = pl.pallas_call(
        spread_kernel,
        compiler_params=SMALL,
        in_specs=[VMEM],
        out_specs=[VMEM] * 2,
        out_shape=[shape(blocks, REACH, 2 * STRIP, HEAD_DIM), shape(ways, 2 * STRIP, HEAD_DIM)],
    )(mine)
    keys = lax.all_to_all(spread, "qrow", 0, 0)
    far = from_partner(qg, 2)
    others = [from_partner(qg, 1), far, from_partner(far, 1)]
    *dq_parts, dkv_part = call_tiles(place, doc_lengths, mine, qg, *others, keys)
    dkv = lax.all_to_all(dkv_part, "qrow", 0, 0)
    dq_parts = [dq_parts[0]] + [from_partner(dq_parts[s], s) for s in range(1, WAYS)]
    sums = pl.pallas_call(
        collect_kernel,
        compiler_params=SMALL,
        in_specs=[VMEM] * 5,
        out_specs=VMEM,
        out_shape=shape(ways, 3 * STRIP, HEAD_DIM),
    )(*dq_parts, dkv)
    back = lax.all_to_all(sums, KCOL, 0, 0)
    width = HEADS * HEAD_DIM
    return tuple(
        pl.pallas_call(
            unpack_kernel,
            compiler_params=SMALL,
            in_specs=[VMEM],
            out_specs=[VMEM] * 3,
            out_shape=[shape(CHUNK, width)] * 3,
        )(back)
    )


def solution(mesh):
    finer = Mesh(mesh.devices.reshape(mesh.shape["qrow"], HEADS, WAYS), ("qrow",) + KCOL)
    rows = P(("qrow",) + KCOL, None)
    keys = P(KCOL + ("qrow",), None)
    return jax.shard_map(
        per_device,
        mesh=finer,
        in_specs=(rows, keys, keys, rows, rows, rows, P()),
        out_specs=(rows, keys, keys),
        check_vma=False,
    )
```

```python
import math

import jax
import jax.numpy as jnp
from jax import lax
from jax.experimental import pallas as pl
from jax.experimental.pallas import tpu as pltpu
from jax.sharding import Mesh
from jax.sharding import PartitionSpec as P

HEAD_DIM = 128
HEADS = 4
BLOCK = 2048
CHUNK = 128
WAYS = 4
STRIP = CHUNK // WAYS
REACH = 5
KSPAN = 2048
KROWS = KSPAN // WAYS
QROWS = 512
SCALE = HEAD_DIM**-0.5
LOG2E = math.log2(math.e)
EXTRA = 8
OFF_DO = STRIP
OFF_K = 2 * STRIP
OFF_V = 3 * STRIP
OFF_EXTRA = 4 * STRIP
PACKED = OFF_EXTRA + EXTRA
KCOL = ("kcol_h", "kcol_s")
STRIPS = "kcol_s"
F32 = jnp.float32
BF16 = jnp.bfloat16
VMEM = pl.BlockSpec(memory_space=pltpu.VMEM)
SMALL = pltpu.CompilerParams(vmem_limit_bytes=8 * 1024 * 1024)
SMEM = pl.BlockSpec(memory_space=pltpu.SMEM)


def pieces(x):
    high = x.astype(BF16)
    rest = x - high.astype(F32)
    middle = rest.astype(BF16)
    low = (rest - middle.astype(F32)).astype(BF16)
    return [high, middle, low]


def head_and_strip(t):
    return t // WAYS, t % WAYS


def pack_kernel(q_ref, k_ref, v_ref, o_ref, g_ref, n_ref, out_ref):
    norms = n_ref[...] * LOG2E
    ones = jnp.ones((8, HEAD_DIM), F32)
    extras = []
    for h in range(HEADS):
        at = slice(h * HEAD_DIM, (h + 1) * HEAD_DIM)
        delta = lax.dot_general(
            ones, g_ref[:, at].astype(F32) * o_ref[:, at].astype(F32), (((1,), (1,)), ((), ())),
            precision=lax.Precision.HIGHEST, preferred_element_type=F32,
        )[:1]
        extras.append(
            jnp.concatenate(
                [p.astype(F32) for p in pieces(norms[h : h + 1]) + pieces(delta)]
                + [jnp.zeros((EXTRA - 6, CHUNK), F32)], axis=0
            )
        )
    for t in range(out_ref.shape[0]):
        h, d = head_and_strip(t)
        at = slice(h * HEAD_DIM, (h + 1) * HEAD_DIM)
        rows = slice(d * STRIP, (d + 1) * STRIP)
        out_ref[t, 0:STRIP] = q_ref[rows, at]
        out_ref[t, OFF_DO : OFF_DO + STRIP] = g_ref[rows, at]
        out_ref[t, OFF_K : OFF_K + STRIP] = k_ref[rows, at]
        out_ref[t, OFF_V : OFF_V + STRIP] = v_ref[rows, at]
        order = [extras[h][:, (d ^ s) * STRIP : (d ^ s) * STRIP + STRIP] for s in range(WAYS)]
        out_ref[t, OFF_EXTRA:PACKED] = jnp.concatenate(order, axis=1).astype(BF16)


def spread_kernel(in_ref, out_ref, qg_ref):
    count = out_ref.shape[0]
    qg_ref[...] = in_ref[:, 0 : 2 * STRIP]
    for b in range(count):
        for back in range(REACH):
            out_ref[b, back] = in_ref[max(b - back, 0), OFF_K : OFF_K + 2 * STRIP]


def tiles(half, place_ref, lengths_ref, in_ref, qg_refs, kv_ref, dq_refs, dk_acc, dv_acc, dq_acc, q_all, g_all):
    block = place_ref[0]
    strip = place_ref[1]
    ends = []
    total = jnp.int32(0)
    for e in range(lengths_ref.shape[0]):
        total = total + lengths_ref[e]
        ends.append(total)
    base = (block - (REACH - 1)) * BLOCK
    for i, ref in enumerate(qg_refs):
        q_all[:, i] = ref[:, 0:STRIP]
        g_all[:, i] = ref[:, STRIP : 2 * STRIP]
    dk_acc[...] = jnp.zeros_like(dk_acc)
    dv_acc[...] = jnp.zeros_like(dv_acc)
    j_tile = KROWS // STRIP
    per_block = BLOCK // KSPAN
    k_iota = lax.broadcasted_iota(jnp.int32, (KROWS, 1), 0)
    k_iota = (k_iota // STRIP) * CHUNK + k_iota % STRIP + strip * STRIP
    for t in range(2 * STRIP * in_ref.shape[0] // QROWS):
        query_tile(half, t, block, strip, ends, base, k_iota, in_ref, kv_ref, dq_refs, dk_acc, dv_acc, dq_acc, q_all, g_all)


def query_tile(
    half, t, block, strip, ends, base, k_iota, in_ref, kv_ref, dq_refs, dk_acc, dv_acc, dq_acc, q_all, g_all
):
    width = 2 * STRIP
    sources = QROWS // width
    ms = slice(t * sources, (t + 1) * sources)
    span = sources * CHUNK
    j_tile = KROWS // STRIP
    per_block = BLOCK // KSPAN
    dq_acc[...] = jnp.zeros_like(dq_acc)
    first = block * BLOCK + t * span
    last = first + span - 1
    lane = lax.broadcasted_iota(jnp.int32, (1, QROWS), 1)
    strips = [strip ^ (2 * half), strip ^ (2 * half + 1)]
    q_pos = first + lane // width * CHUNK + lane % STRIP
    q_pos = q_pos + jnp.where(lane // STRIP % 2 == 0, strips[0], strips[1]) * STRIP
    q_doc = jnp.zeros((1, QROWS), jnp.int32)
    doc_first = jnp.int32(0)
    doc_last = jnp.int32(0)
    for end in ends:
        doc_first = jnp.where(end <= first, end, doc_first)
        doc_last = jnp.where(end <= last, end, doc_last)
        q_doc = jnp.where(end <= q_pos, end, q_doc)
    low = (doc_first - base) // KSPAN
    high = (last - base) // KSPAN
    q = q_all[ms].reshape(QROWS, HEAD_DIM)
    g = g_all[ms].reshape(QROWS, HEAD_DIM)

    def row(at):
        values = []
        for m in range(t * sources, (t + 1) * sources):
            e = in_ref[m, OFF_EXTRA:PACKED, half * width : (half + 1) * width].astype(F32)
            values.append(e[at : at + 1] + e[at + 1 : at + 2] + e[at + 2 : at + 3])
        return jnp.concatenate(values, axis=1)

    norm, delta = row(0), row(3)

    def one_tile(kt, masked):
        js = pl.ds((kt % per_block) * j_tile, j_tile)
        back = REACH - 1 - kt // per_block
        k = kv_ref[js, back, 0:STRIP].reshape(KROWS, HEAD_DIM)
        v = kv_ref[js, back, STRIP : 2 * STRIP].reshape(KROWS, HEAD_DIM)
        across = (((1,), (1,)), ((), ()))
        s = lax.dot_general(k, q, across, preferred_element_type=F32)
        p = jnp.exp2(s * (SCALE * LOG2E) - norm)
        if masked:
            k_pos = k_iota + (base + kt * KSPAN)
            p = jnp.where((k_pos <= q_pos) & (k_pos >= q_doc), p, 0.0)
        dp = lax.dot_general(v, g, across, preferred_element_type=F32)
        ds = (p * (dp - delta)).astype(BF16)
        p = p.astype(BF16)
        dv_acc[kt] += jnp.dot(p, g, preferred_element_type=F32)
        dk_acc[kt] += jnp.dot(ds, q, preferred_element_type=F32)
        dq_acc[...] += lax.dot_general(
            k, ds, (((0,), (0,)), ((), ())), preferred_element_type=F32
        )

    def key_tile(kt, carry):
        start = base + kt * KSPAN
        whole = (start + KSPAN - 1 <= first) & (start >= doc_last)

        @pl.when(whole)
        def _():
            one_tile(kt, False)

        @pl.when(jnp.logical_not(whole))
        def _():
            one_tile(kt, True)

        return carry

    lax.fori_loop(low, high + 1, key_tile, 0)
    dq = (dq_acc[...].T * SCALE).astype(BF16).reshape(sources, 2, STRIP, HEAD_DIM)
    for i, ref in enumerate(dq_refs):
        ref[ms] = dq[:, i]


def first_kernel(
    place_ref, lengths_ref, in_ref, qg0, qg1, kv_ref,
    dq0, dq1, dk_acc, dv_acc, dq_acc, q_all, g_all,
):
    tiles(0, place_ref, lengths_ref, in_ref, (qg0, qg1), kv_ref, (dq0, dq1), dk_acc, dv_acc, dq_acc, q_all, g_all)


def second_kernel(
    place_ref, lengths_ref, in_ref, qg2, qg3, kv_ref, dk_in, dv_in,
    dq2, dq3, dkv_ref, dk_acc, dv_acc, dq_acc, q_all, g_all,
):
    tiles(1, place_ref, lengths_ref, in_ref, (qg2, qg3), kv_ref, (dq2, dq3), dk_acc, dv_acc, dq_acc, q_all, g_all)
    j_tile = KROWS // STRIP
    per_block = BLOCK // KSPAN
    for kt in range(REACH * per_block):
        js = slice((kt % per_block) * j_tile, (kt % per_block + 1) * j_tile)
        back = REACH - 1 - kt // per_block
        dk = (dk_acc[kt] + dk_in[kt]) * SCALE
        dv = dv_acc[kt] + dv_in[kt]
        dkv_ref[js, back, 0:STRIP] = dk.astype(BF16).reshape(j_tile, STRIP, HEAD_DIM)
        dkv_ref[js, back, STRIP : 2 * STRIP] = dv.astype(BF16).reshape(j_tile, STRIP, HEAD_DIM)


def collect_kernel(dq0, dq1, dq2, dq3, dkv_ref, out_ref):
    count = out_ref.shape[0]
    dq = dq0[...].astype(F32)
    for ref in (dq1, dq2, dq3):
        dq = dq + ref[...].astype(F32)
    out_ref[:, 0:STRIP] = dq.astype(BF16)
    for b in range(count):
        total = dkv_ref[b, 0].astype(F32)
        for back in range(1, REACH):
            if b + back < count:
                total = total + dkv_ref[b + back, back].astype(F32)
        out_ref[b, STRIP : 3 * STRIP] = total.astype(BF16)


def unpack_kernel(in_ref, dq_ref, dk_ref, dv_ref):
    for t in range(in_ref.shape[0]):
        h, d = head_and_strip(t)
        at = slice(h * HEAD_DIM, (h + 1) * HEAD_DIM)
        rows = slice(d * STRIP, (d + 1) * STRIP)
        dq_ref[rows, at] = in_ref[t, 0:STRIP]
        dk_ref[rows, at] = in_ref[t, STRIP : 2 * STRIP]
        dv_ref[rows, at] = in_ref[t, 2 * STRIP : 3 * STRIP]


def shape(*dims, dtype=BF16):
    return jax.ShapeDtypeStruct(dims, dtype)


def from_partner(x, s):
    return lax.ppermute(x, STRIPS, [(d, d ^ s) for d in range(WAYS)])


def call_tiles(place, doc_lengths, mine, own, near, far, diagonal, keys):
    ways, blocks = mine.shape[0], keys.shape[0]
    sums = (REACH * BLOCK // KSPAN, KROWS, HEAD_DIM)
    scratch = [pltpu.VMEM((HEAD_DIM, QROWS), F32)] + [pltpu.VMEM((ways, 2, STRIP, HEAD_DIM), BF16)] * 2
    params = pltpu.CompilerParams(vmem_limit_bytes=24 * 1024 * 1024)
    dq0, dq1, dk, dv = pl.pallas_call(
        first_kernel,
        in_specs=[SMEM, SMEM] + [VMEM] * 4,
        out_specs=[VMEM] * 4,
        out_shape=[shape(ways, STRIP, HEAD_DIM)] * 2 + [shape(*sums, dtype=F32)] * 2,
        scratch_shapes=scratch,
        compiler_params=params,
    )(place, doc_lengths, mine, own, near, keys)
    dq2, dq3, dkv = pl.pallas_call(
        second_kernel,
        in_specs=[SMEM, SMEM] + [VMEM] * 6,
        out_specs=[VMEM] * 3,
        out_shape=[shape(ways, STRIP, HEAD_DIM)] * 2 + [shape(blocks, REACH, 2 * STRIP, HEAD_DIM)],
        scratch_shapes=[pltpu.VMEM(sums, F32)] * 2 + scratch,
        compiler_params=params,
    )(place, doc_lengths, mine, far, diagonal, keys, dk, dv)
    return dq0, dq1, dq2, dq3, dkv


def per_device(query_states, key_states, value_states, saved_output, output_grad, normalizer, doc_lengths):
    blocks = lax.axis_size("qrow")
    ways = lax.axis_size(KCOL)
    place = jnp.stack([lax.axis_index("qrow"), lax.axis_index(STRIPS)]).astype(jnp.int32)
    packed = pl.pallas_call(
        pack_kernel,
        compiler_params=pltpu.CompilerParams(vmem_limit_bytes=60 * 1024 * 1024),
        in_specs=[VMEM] * 6,
        out_specs=VMEM,
        out_shape=shape(ways, PACKED, HEAD_DIM),
    )(query_states, key_states, value_states, saved_output, output_grad, normalizer.T)
    mine = lax.all_to_all(packed, KCOL, 0, 0)
    spread, qg = pl.pallas_call(
        spread_kernel,
        compiler_params=SMALL,
        in_specs=[VMEM],
        out_specs=[VMEM] * 2,
        out_shape=[shape(blocks, REACH, 2 * STRIP, HEAD_DIM), shape(ways, 2 * STRIP, HEAD_DIM)],
    )(mine)
    keys = lax.all_to_all(spread, "qrow", 0, 0)
    far = from_partner(qg, 2)
    others = [from_partner(qg, 1), far, from_partner(far, 1)]
    *dq_parts, dkv_part = call_tiles(place, doc_lengths, mine, qg, *others, keys)
    dkv = lax.all_to_all(dkv_part, "qrow", 0, 0)
    dq_parts = [dq_parts[0]] + [from_partner(dq_parts[s], s) for s in range(1, WAYS)]
    sums = pl.pallas_call(
        collect_kernel,
        compiler_params=SMALL,
        in_specs=[VMEM] * 5,
        out_specs=VMEM,
        out_shape=shape(ways, 3 * STRIP, HEAD_DIM),
    )(*dq_parts, dkv)
    back = lax.all_to_all(sums, KCOL, 0, 0)
    width = HEADS * HEAD_DIM
    return tuple(
        pl.pallas_call(
            unpack_kernel,
            compiler_params=SMALL,
            in_specs=[VMEM],
            out_specs=[VMEM] * 3,
            out_shape=[shape(CHUNK, width)] * 3,
        )(back)
    )


def solution(mesh):
    finer = Mesh(mesh.devices.reshape(mesh.shape["qrow"], HEADS, WAYS), ("qrow",) + KCOL)
    rows = P(("qrow",) + KCOL, None)
    keys = P(KCOL + ("qrow",), None)
    return jax.shard_map(
        per_device,
        mesh=finer,
        in_specs=(rows, keys, keys, rows, rows, rows, P()),
        out_specs=(rows, keys, keys),
        check_vma=False,
    )
```

```python
import math

import jax
import jax.numpy as jnp
from jax import lax
from jax.experimental import pallas as pl
from jax.experimental.pallas import tpu as pltpu
from jax.sharding import Mesh
from jax.sharding import PartitionSpec as P

HEAD_DIM = 128
HEADS = 4
BLOCK = 2048
CHUNK = 128
WAYS = 4
STRIP = CHUNK // WAYS
REACH = 5
KSPAN = 2048
KROWS = KSPAN // WAYS
QROWS = 512
SCALE = HEAD_DIM**-0.5
LOG2E = math.log2(math.e)
EXTRA = 8
OFF_DO = STRIP
OFF_K = 2 * STRIP
OFF_V = 3 * STRIP
OFF_EXTRA = 4 * STRIP
PACKED = OFF_EXTRA + EXTRA
KCOL = ("kcol_h", "kcol_s")
STRIPS = "kcol_s"
F32 = jnp.float32
BF16 = jnp.bfloat16
VMEM = pl.BlockSpec(memory_space=pltpu.VMEM)
SMALL = pltpu.CompilerParams(vmem_limit_bytes=8 * 1024 * 1024)
SMEM = pl.BlockSpec(memory_space=pltpu.SMEM)


def pieces(x):
    high = x.astype(BF16)
    rest = x - high.astype(F32)
    middle = rest.astype(BF16)
    low = (rest - middle.astype(F32)).astype(BF16)
    return [high, middle, low]


def head_and_strip(t):
    return t // WAYS, t % WAYS


def pack_kernel(q_ref, k_ref, v_ref, o_ref, g_ref, n_ref, out_ref):
    norms = n_ref[...] * LOG2E
    ones = jnp.ones((8, HEAD_DIM), F32)
    extras = []
    for h in range(HEADS):
        at = slice(h * HEAD_DIM, (h + 1) * HEAD_DIM)
        delta = lax.dot_general(
            ones, g_ref[:, at].astype(F32) * o_ref[:, at].astype(F32), (((1,), (1,)), ((), ())),
            precision=lax.Precision.HIGHEST, preferred_element_type=F32,
        )[:1]
        extras.append(
            jnp.concatenate(
                [p.astype(F32) for p in pieces(norms[h : h + 1]) + pieces(delta)]
                + [jnp.zeros((EXTRA - 6, CHUNK), F32)], axis=0
            )
        )
    for t in range(out_ref.shape[0]):
        h, d = head_and_strip(t)
        at = slice(h * HEAD_DIM, (h + 1) * HEAD_DIM)
        rows = slice(d * STRIP, (d + 1) * STRIP)
        out_ref[t, 0:STRIP] = q_ref[rows, at]
        out_ref[t, OFF_DO : OFF_DO + STRIP] = g_ref[rows, at]
        out_ref[t, OFF_K : OFF_K + STRIP] = k_ref[rows, at]
        out_ref[t, OFF_V : OFF_V + STRIP] = v_ref[rows, at]
        order = [extras[h][:, (d ^ s) * STRIP : (d ^ s) * STRIP + STRIP] for s in range(WAYS)]
        out_ref[t, OFF_EXTRA:PACKED] = jnp.concatenate(order, axis=1).astype(BF16)


def spread_kernel(in_ref, out_ref, qg_ref):
    count = out_ref.shape[0]
    qg_ref[...] = in_ref[:, 0 : 2 * STRIP]
    for b in range(count):
        for back in range(REACH):
            out_ref[b, back] = in_ref[max(b - back, 0), OFF_K : OFF_K + 2 * STRIP]


def tiles(half, place_ref, lengths_ref, in_ref, qg_refs, kv_ref, dq_refs, dk_acc, dv_acc, dq_acc, q_all, g_all):
    block = place_ref[0]
    strip = place_ref[1]
    ends = []
    total = jnp.int32(0)
    for e in range(lengths_ref.shape[0]):
        total = total + lengths_ref[e]
        ends.append(total)
    base = (block - (REACH - 1)) * BLOCK
    for i, ref in enumerate(qg_refs):
        q_all[:, i] = ref[:, 0:STRIP]
        g_all[:, i] = ref[:, STRIP : 2 * STRIP]
    j_tile = KROWS // STRIP
    per_block = BLOCK // KSPAN
    k_iota = lax.broadcasted_iota(jnp.int32, (KROWS, 1), 0)
    k_iota = (k_iota // STRIP) * CHUNK + k_iota % STRIP + strip * STRIP
    for t in range(2 * STRIP * in_ref.shape[0] // QROWS):
        query_tile(half, t, block, strip, ends, base, k_iota, in_ref, kv_ref, dq_refs, dk_acc, dv_acc, dq_acc, q_all, g_all)


def query_tile(
    half, t, block, strip, ends, base, k_iota, in_ref, kv_ref, dq_refs, dk_acc, dv_acc, dq_acc, q_all, g_all
):
    width = 2 * STRIP
    sources = QROWS // width
    ms = slice(t * sources, (t + 1) * sources)
    span = sources * CHUNK
    j_tile = KROWS // STRIP
    per_block = BLOCK // KSPAN
    dq_acc[...] = jnp.zeros_like(dq_acc)
    first = block * BLOCK + t * span
    last = first + span - 1
    lane = lax.broadcasted_iota(jnp.int32, (1, QROWS), 1)
    strips = [strip ^ (2 * half), strip ^ (2 * half + 1)]
    q_pos = first + lane // width * CHUNK + lane % STRIP
    q_pos = q_pos + jnp.where(lane // STRIP % 2 == 0, strips[0], strips[1]) * STRIP
    q_doc = jnp.zeros((1, QROWS), jnp.int32)
    doc_first = jnp.int32(0)
    doc_last = jnp.int32(0)
    for end in ends:
        doc_first = jnp.where(end <= first, end, doc_first)
        doc_last = jnp.where(end <= last, end, doc_last)
        q_doc = jnp.where(end <= q_pos, end, q_doc)
    low = (doc_first - base) // KSPAN
    high = (last - base) // KSPAN
    q = q_all[ms].reshape(QROWS, HEAD_DIM)
    g = g_all[ms].reshape(QROWS, HEAD_DIM)

    def row(at):
        values = []
        for m in range(t * sources, (t + 1) * sources):
            e = in_ref[m, OFF_EXTRA:PACKED, half * width : (half + 1) * width].astype(F32)
            values.append(e[at : at + 1] + e[at + 1 : at + 2] + e[at + 2 : at + 3])
        return jnp.concatenate(values, axis=1)

    norm, delta = row(0), row(3)

    def one_tile(kt, masked):
        js = pl.ds((kt % per_block) * j_tile, j_tile)
        back = REACH - 1 - kt // per_block
        k = kv_ref[js, back, 0:STRIP].reshape(KROWS, HEAD_DIM)
        v = kv_ref[js, back, STRIP : 2 * STRIP].reshape(KROWS, HEAD_DIM)
        across = (((1,), (1,)), ((), ()))
        s = lax.dot_general(k, q, across, preferred_element_type=F32)
        p = jnp.exp2(s * (SCALE * LOG2E) - norm)
        if masked:
            k_pos = k_iota + (base + kt * KSPAN)
            p = jnp.where((k_pos <= q_pos) & (k_pos >= q_doc), p, 0.0)
        dp = lax.dot_general(v, g, across, preferred_element_type=F32)
        ds = (p * (dp - delta)).astype(BF16)
        p = p.astype(BF16)
        dv_acc[kt] += jnp.dot(p, g, preferred_element_type=F32)
        dk_acc[kt] += jnp.dot(ds, q, preferred_element_type=F32)
        dq_acc[...] += lax.dot_general(
            k, ds, (((0,), (0,)), ((), ())), preferred_element_type=F32
        )

    def key_tile(kt, carry):
        start = base + kt * KSPAN
        whole = (start + KSPAN - 1 <= first) & (start >= doc_last)

        @pl.when(whole)
        def _():
            one_tile(kt, False)

        @pl.when(jnp.logical_not(whole))
        def _():
            one_tile(kt, True)

        return carry

    lax.fori_loop(low, high + 1, key_tile, 0)
    dq = (dq_acc[...].T * SCALE).astype(BF16).reshape(sources, 2, STRIP, HEAD_DIM)
    for i, ref in enumerate(dq_refs):
        ref[ms] = dq[:, i]


def first_kernel(
    place_ref, lengths_ref, in_ref, qg0, qg1, kv_ref,
    dq0, dq1, dk_acc, dv_acc, dq_acc, q_all, g_all,
):
    dk_acc[...] = jnp.zeros_like(dk_acc)
    dv_acc[...] = jnp.zeros_like(dv_acc)
    tiles(0, place_ref, lengths_ref, in_ref, (qg0, qg1), kv_ref, (dq0, dq1), dk_acc, dv_acc, dq_acc, q_all, g_all)


def second_kernel(
    place_ref, lengths_ref, in_ref, qg2, qg3, kv_ref, dk_in, dv_in,
    dq2, dq3, dkv_ref, dk_acc, dv_acc, dq_acc, q_all, g_all,
):
    dk_acc[...] = dk_in[...]
    dv_acc[...] = dv_in[...]
    tiles(1, place_ref, lengths_ref, in_ref, (qg2, qg3), kv_ref, (dq2, dq3), dk_acc, dv_acc, dq_acc, q_all, g_all)
    j_tile = KROWS // STRIP
    per_block = BLOCK // KSPAN
    for kt in range(REACH * per_block):
        js = slice((kt % per_block) * j_tile, (kt % per_block + 1) * j_tile)
        back = REACH - 1 - kt // per_block
        dk = dk_acc[kt] * SCALE
        dv = dv_acc[kt]
        dkv_ref[js, back, 0:STRIP] = dk.astype(BF16).reshape(j_tile, STRIP, HEAD_DIM)
        dkv_ref[js, back, STRIP : 2 * STRIP] = dv.astype(BF16).reshape(j_tile, STRIP, HEAD_DIM)


def collect_kernel(dq0, dq1, dq2, dq3, dkv_ref, out_ref):
    count = out_ref.shape[0]
    dq = dq0[...].astype(F32)
    for ref in (dq1, dq2, dq3):
        dq = dq + ref[...].astype(F32)
    out_ref[:, 0:STRIP] = dq.astype(BF16)
    for b in range(count):
        total = dkv_ref[b, 0].astype(F32)
        for back in range(1, REACH):
            if b + back < count:
                total = total + dkv_ref[b + back, back].astype(F32)
        out_ref[b, STRIP : 3 * STRIP] = total.astype(BF16)


def unpack_kernel(in_ref, dq_ref, dk_ref, dv_ref):
    for t in range(in_ref.shape[0]):
        h, d = head_and_strip(t)
        at = slice(h * HEAD_DIM, (h + 1) * HEAD_DIM)
        rows = slice(d * STRIP, (d + 1) * STRIP)
        dq_ref[rows, at] = in_ref[t, 0:STRIP]
        dk_ref[rows, at] = in_ref[t, STRIP : 2 * STRIP]
        dv_ref[rows, at] = in_ref[t, 2 * STRIP : 3 * STRIP]


def shape(*dims, dtype=BF16):
    return jax.ShapeDtypeStruct(dims, dtype)


def from_partner(x, s):
    return lax.ppermute(x, STRIPS, [(d, d ^ s) for d in range(WAYS)])


def call_tiles(place, doc_lengths, mine, own, near, far, diagonal, keys):
    ways, blocks = mine.shape[0], keys.shape[0]
    sums = (REACH * BLOCK // KSPAN, KROWS, HEAD_DIM)
    scratch = [pltpu.VMEM((HEAD_DIM, QROWS), F32)] + [pltpu.VMEM((ways, 2, STRIP, HEAD_DIM), BF16)] * 2
    params = pltpu.CompilerParams(vmem_limit_bytes=24 * 1024 * 1024)
    dq0, dq1, dk, dv = pl.pallas_call(
        first_kernel,
        in_specs=[SMEM, SMEM] + [VMEM] * 4,
        out_specs=[VMEM] * 4,
        out_shape=[shape(ways, STRIP, HEAD_DIM)] * 2 + [shape(*sums, dtype=F32)] * 2,
        scratch_shapes=scratch,
        compiler_params=params,
    )(place, doc_lengths, mine, own, near, keys)
    dq2, dq3, dkv = pl.pallas_call(
        second_kernel,
        in_specs=[SMEM, SMEM] + [VMEM] * 6,
        out_specs=[VMEM] * 3,
        out_shape=[shape(ways, STRIP, HEAD_DIM)] * 2 + [shape(blocks, REACH, 2 * STRIP, HEAD_DIM)],
        scratch_shapes=[pltpu.VMEM(sums, F32)] * 2 + scratch,
        compiler_params=params,
    )(place, doc_lengths, mine, far, diagonal, keys, dk, dv)
    return dq0, dq1, dq2, dq3, dkv


def per_device(query_states, key_states, value_states, saved_output, output_grad, normalizer, doc_lengths):
    blocks = lax.axis_size("qrow")
    ways = lax.axis_size(KCOL)
    place = jnp.stack([lax.axis_index("qrow"), lax.axis_index(STRIPS)]).astype(jnp.int32)
    packed = pl.pallas_call(
        pack_kernel,
        compiler_params=pltpu.CompilerParams(vmem_limit_bytes=60 * 1024 * 1024),
        in_specs=[VMEM] * 6,
        out_specs=VMEM,
        out_shape=shape(ways, PACKED, HEAD_DIM),
    )(query_states, key_states, value_states, saved_output, output_grad, normalizer.T)
    mine = lax.all_to_all(packed, KCOL, 0, 0)
    spread, qg = pl.pallas_call(
        spread_kernel,
        compiler_params=SMALL,
        in_specs=[VMEM],
        out_specs=[VMEM] * 2,
        out_shape=[shape(blocks, REACH, 2 * STRIP, HEAD_DIM), shape(ways, 2 * STRIP, HEAD_DIM)],
    )(mine)
    keys = lax.all_to_all(spread, "qrow", 0, 0)
    far = from_partner(qg, 2)
    others = [from_partner(qg, 1), far, from_partner(far, 1)]
    *dq_parts, dkv_part = call_tiles(place, doc_lengths, mine, qg, *others, keys)
    dkv = lax.all_to_all(dkv_part, "qrow", 0, 0)
    dq_parts = [dq_parts[0]] + [from_partner(dq_parts[s], s) for s in range(1, WAYS)]
    sums = pl.pallas_call(
        collect_kernel,
        compiler_params=SMALL,
        in_specs=[VMEM] * 5,
        out_specs=VMEM,
        out_shape=shape(ways, 3 * STRIP, HEAD_DIM),
    )(*dq_parts, dkv)
    back = lax.all_to_all(sums, KCOL, 0, 0)
    width = HEADS * HEAD_DIM
    return tuple(
        pl.pallas_call(
            unpack_kernel,
            compiler_params=SMALL,
            in_specs=[VMEM],
            out_specs=[VMEM] * 3,
            out_shape=[shape(CHUNK, width)] * 3,
        )(back)
    )


def solution(mesh):
    finer = Mesh(mesh.devices.reshape(mesh.shape["qrow"], HEADS, WAYS), ("qrow",) + KCOL)
    rows = P(("qrow",) + KCOL, None)
    keys = P(KCOL + ("qrow",), None)
    return jax.shard_map(
        per_device,
        mesh=finer,
        in_specs=(rows, keys, keys, rows, rows, rows, P()),
        out_specs=(rows, keys, keys),
        check_vma=False,
    )
```

```python
import math

import jax
import jax.numpy as jnp
from jax import lax
from jax.experimental import pallas as pl
from jax.experimental.pallas import tpu as pltpu
from jax.sharding import Mesh
from jax.sharding import PartitionSpec as P

HEAD_DIM = 128
HEADS = 4
BLOCK = 2048
CHUNK = 128
WAYS = 4
STRIP = CHUNK // WAYS
REACH = 5
KSPAN = 2048
KROWS = KSPAN // WAYS
QROWS = 512
SCALE = HEAD_DIM**-0.5
LOG2E = math.log2(math.e)
EXTRA = 8
OFF_DO = STRIP
OFF_K = 2 * STRIP
OFF_V = 3 * STRIP
OFF_EXTRA = 4 * STRIP
PACKED = OFF_EXTRA + EXTRA
KCOL = ("kcol_h", "kcol_s")
STRIPS = "kcol_s"
F32 = jnp.float32
BF16 = jnp.bfloat16
VMEM = pl.BlockSpec(memory_space=pltpu.VMEM)
SMALL = pltpu.CompilerParams(vmem_limit_bytes=8 * 1024 * 1024)
SMEM = pl.BlockSpec(memory_space=pltpu.SMEM)


def pieces(x):
    high = x.astype(BF16)
    rest = x - high.astype(F32)
    middle = rest.astype(BF16)
    low = (rest - middle.astype(F32)).astype(BF16)
    return [high, middle, low]


def head_and_strip(t):
    return t // WAYS, t % WAYS


def pack_kernel(q_ref, k_ref, v_ref, o_ref, g_ref, n_ref, out_ref):
    norms = n_ref[...] * LOG2E
    ones = jnp.ones((8, HEAD_DIM), F32)
    extras = []
    for h in range(HEADS):
        at = slice(h * HEAD_DIM, (h + 1) * HEAD_DIM)
        delta = lax.dot_general(
            ones, g_ref[:, at].astype(F32) * o_ref[:, at].astype(F32), (((1,), (1,)), ((), ())),
            precision=lax.Precision.HIGHEST, preferred_element_type=F32,
        )[:1]
        extras.append(
            jnp.concatenate(
                [p.astype(F32) for p in pieces(norms[h : h + 1]) + pieces(delta)]
                + [jnp.zeros((EXTRA - 6, CHUNK), F32)], axis=0
            )
        )
    for t in range(out_ref.shape[0]):
        h, d = head_and_strip(t)
        at = slice(h * HEAD_DIM, (h + 1) * HEAD_DIM)
        rows = slice(d * STRIP, (d + 1) * STRIP)
        out_ref[t, 0:STRIP] = q_ref[rows, at]
        out_ref[t, OFF_DO : OFF_DO + STRIP] = g_ref[rows, at]
        out_ref[t, OFF_K : OFF_K + STRIP] = k_ref[rows, at]
        out_ref[t, OFF_V : OFF_V + STRIP] = v_ref[rows, at]
        order = [extras[h][:, (d ^ s) * STRIP : (d ^ s) * STRIP + STRIP] for s in range(WAYS)]
        out_ref[t, OFF_EXTRA:PACKED] = jnp.concatenate(order, axis=1).astype(BF16)


def spread_kernel(in_ref, out_ref, qg_ref):
    count = out_ref.shape[0]
    qg_ref[...] = in_ref[:, 0 : 2 * STRIP]
    for b in range(count):
        for back in range(REACH):
            out_ref[b, back] = in_ref[max(b - back, 0), OFF_K : OFF_K + 2 * STRIP]


def tiles(half, place_ref, lengths_ref, in_ref, qg_refs, kv_ref, dq_refs, dk_acc, dv_acc, dq_acc, q_all, g_all):
    block = place_ref[0]
    strip = place_ref[1]
    ends = []
    total = jnp.int32(0)
    for e in range(lengths_ref.shape[0]):
        total = total + lengths_ref[e]
        ends.append(total)
    base = (block - (REACH - 1)) * BLOCK
    for i, ref in enumerate(qg_refs):
        q_all[:, i] = ref[:, 0:STRIP]
        g_all[:, i] = ref[:, STRIP : 2 * STRIP]
    j_tile = KROWS // STRIP
    per_block = BLOCK // KSPAN
    k_iota = lax.broadcasted_iota(jnp.int32, (KROWS, 1), 0)
    k_iota = (k_iota // STRIP) * CHUNK + k_iota % STRIP + strip * STRIP
    for t in range(2 * STRIP * in_ref.shape[0] // QROWS):
        query_tile(half, t, block, strip, ends, base, k_iota, in_ref, kv_ref, dq_refs, dk_acc, dv_acc, dq_acc, q_all, g_all)


def query_tile(
    half, t, block, strip, ends, base, k_iota, in_ref, kv_ref, dq_refs, dk_acc, dv_acc, dq_acc, q_all, g_all
):
    width = 2 * STRIP
    sources = QROWS // width
    ms = slice(t * sources, (t + 1) * sources)
    span = sources * CHUNK
    j_tile = KROWS // STRIP
    per_block = BLOCK // KSPAN
    dq_acc[...] = jnp.zeros_like(dq_acc)
    first = block * BLOCK + t * span
    last = first + span - 1
    lane = lax.broadcasted_iota(jnp.int32, (1, QROWS), 1)
    strips = [strip ^ (2 * half), strip ^ (2 * half + 1)]
    q_pos = first + lane // width * CHUNK + lane % STRIP
    q_pos = q_pos + jnp.where(lane // STRIP % 2 == 0, strips[0], strips[1]) * STRIP
    q_doc = jnp.zeros((1, QROWS), jnp.int32)
    doc_first = jnp.int32(0)
    doc_last = jnp.int32(0)
    for end in ends:
        doc_first = jnp.where(end <= first, end, doc_first)
        doc_last = jnp.where(end <= last, end, doc_last)
        q_doc = jnp.where(end <= q_pos, end, q_doc)
    low = (doc_first - base) // KSPAN
    q = q_all[ms].reshape(QROWS, HEAD_DIM)
    g = g_all[ms].reshape(QROWS, HEAD_DIM)

    def row(at):
        values = []
        for m in range(t * sources, (t + 1) * sources):
            e = in_ref[m, OFF_EXTRA:PACKED, half * width : (half + 1) * width].astype(F32)
            values.append(e[at : at + 1] + e[at + 1 : at + 2] + e[at + 2 : at + 3])
        return jnp.concatenate(values, axis=1)

    norm, delta = row(0), row(3)

    def one_tile(kt, masked, rows=KROWS):
        js = pl.ds((kt % per_block) * j_tile, rows // STRIP)
        back = REACH - 1 - kt // per_block
        k = kv_ref[js, back, 0:STRIP].reshape(rows, HEAD_DIM)
        v = kv_ref[js, back, STRIP : 2 * STRIP].reshape(rows, HEAD_DIM)
        across = (((1,), (1,)), ((), ()))
        s = lax.dot_general(k, q, across, preferred_element_type=F32)
        p = jnp.exp2(s * (SCALE * LOG2E) - norm)
        if masked:
            k_pos = k_iota[:rows] + (base + kt * KSPAN)
            p = jnp.where((k_pos <= q_pos) & (k_pos >= q_doc), p, 0.0)
        dp = lax.dot_general(v, g, across, preferred_element_type=F32)
        ds = (p * (dp - delta)).astype(BF16)
        p = p.astype(BF16)
        dv_acc[kt, 0:rows] += jnp.dot(p, g, preferred_element_type=F32)
        dk_acc[kt, 0:rows] += jnp.dot(ds, q, preferred_element_type=F32)
        dq_acc[...] += lax.dot_general(
            k, ds, (((0,), (0,)), ((), ())), preferred_element_type=F32
        )

    def key_tile(kt, carry):
        start = base + kt * KSPAN
        whole = (start + KSPAN - 1 <= first) & (start >= doc_last)

        @pl.when(whole)
        def _():
            one_tile(kt, False)

        @pl.when(jnp.logical_not(whole))
        def _():
            one_tile(kt, True)

        return carry

    own = REACH * per_block - 1
    lax.fori_loop(low, own, key_tile, 0)
    one_tile(own, True, (t + 1) * span // WAYS)
    dq = (dq_acc[...].T * SCALE).astype(BF16).reshape(sources, 2, STRIP, HEAD_DIM)
    for i, ref in enumerate(dq_refs):
        ref[ms] = dq[:, i]


def first_kernel(
    place_ref, lengths_ref, in_ref, qg0, qg1, kv_ref,
    dq0, dq1, dk_acc, dv_acc, dq_acc, q_all, g_all,
):
    dk_acc[...] = jnp.zeros_like(dk_acc)
    dv_acc[...] = jnp.zeros_like(dv_acc)
    tiles(0, place_ref, lengths_ref, in_ref, (qg0, qg1), kv_ref, (dq0, dq1), dk_acc, dv_acc, dq_acc, q_all, g_all)


def second_kernel(
    place_ref, lengths_ref, in_ref, qg2, qg3, kv_ref, dk_in, dv_in,
    dq2, dq3, dkv_ref, dk_acc, dv_acc, dq_acc, q_all, g_all,
):
    dk_acc[...] = dk_in[...]
    dv_acc[...] = dv_in[...]
    tiles(1, place_ref, lengths_ref, in_ref, (qg2, qg3), kv_ref, (dq2, dq3), dk_acc, dv_acc, dq_acc, q_all, g_all)
    j_tile = KROWS // STRIP
    per_block = BLOCK // KSPAN
    for kt in range(REACH * per_block):
        js = slice((kt % per_block) * j_tile, (kt % per_block + 1) * j_tile)
        back = REACH - 1 - kt // per_block
        dk = dk_acc[kt] * SCALE
        dv = dv_acc[kt]
        dkv_ref[js, back, 0:STRIP] = dk.astype(BF16).reshape(j_tile, STRIP, HEAD_DIM)
        dkv_ref[js, back, STRIP : 2 * STRIP] = dv.astype(BF16).reshape(j_tile, STRIP, HEAD_DIM)


def collect_kernel(dq0, dq1, dq2, dq3, dkv_ref, out_ref):
    count = out_ref.shape[0]
    dq = dq0[...].astype(F32)
    for ref in (dq1, dq2, dq3):
        dq = dq + ref[...].astype(F32)
    out_ref[:, 0:STRIP] = dq.astype(BF16)
    for b in range(count):
        total = dkv_ref[b, 0].astype(F32)
        for back in range(1, REACH):
            if b + back < count:
                total = total + dkv_ref[b + back, back].astype(F32)
        out_ref[b, STRIP : 3 * STRIP] = total.astype(BF16)


def unpack_kernel(in_ref, dq_ref, dk_ref, dv_ref):
    for t in range(in_ref.shape[0]):
        h, d = head_and_strip(t)
        at = slice(h * HEAD_DIM, (h + 1) * HEAD_DIM)
        rows = slice(d * STRIP, (d + 1) * STRIP)
        dq_ref[rows, at] = in_ref[t, 0:STRIP]
        dk_ref[rows, at] = in_ref[t, STRIP : 2 * STRIP]
        dv_ref[rows, at] = in_ref[t, 2 * STRIP : 3 * STRIP]


def shape(*dims, dtype=BF16):
    return jax.ShapeDtypeStruct(dims, dtype)


def from_partner(x, s):
    return lax.ppermute(x, STRIPS, [(d, d ^ s) for d in range(WAYS)])


def call_tiles(place, doc_lengths, mine, own, near, far, diagonal, keys):
    ways, blocks = mine.shape[0], keys.shape[0]
    sums = (REACH * BLOCK // KSPAN, KROWS, HEAD_DIM)
    scratch = [pltpu.VMEM((HEAD_DIM, QROWS), F32)] + [pltpu.VMEM((ways, 2, STRIP, HEAD_DIM), BF16)] * 2
    params = pltpu.CompilerParams(vmem_limit_bytes=24 * 1024 * 1024)
    dq0, dq1, dk, dv = pl.pallas_call(
        first_kernel,
        in_specs=[SMEM, SMEM] + [VMEM] * 4,
        out_specs=[VMEM] * 4,
        out_shape=[shape(ways, STRIP, HEAD_DIM)] * 2 + [shape(*sums, dtype=F32)] * 2,
        scratch_shapes=scratch,
        compiler_params=params,
    )(place, doc_lengths, mine, own, near, keys)
    dq2, dq3, dkv = pl.pallas_call(
        second_kernel,
        in_specs=[SMEM, SMEM] + [VMEM] * 6,
        out_specs=[VMEM] * 3,
        out_shape=[shape(ways, STRIP, HEAD_DIM)] * 2 + [shape(blocks, REACH, 2 * STRIP, HEAD_DIM)],
        scratch_shapes=[pltpu.VMEM(sums, F32)] * 2 + scratch,
        compiler_params=params,
    )(place, doc_lengths, mine, far, diagonal, keys, dk, dv)
    return dq0, dq1, dq2, dq3, dkv


def per_device(query_states, key_states, value_states, saved_output, output_grad, normalizer, doc_lengths):
    blocks = lax.axis_size("qrow")
    ways = lax.axis_size(KCOL)
    place = jnp.stack([lax.axis_index("qrow"), lax.axis_index(STRIPS)]).astype(jnp.int32)
    packed = pl.pallas_call(
        pack_kernel,
        compiler_params=pltpu.CompilerParams(vmem_limit_bytes=60 * 1024 * 1024),
        in_specs=[VMEM] * 6,
        out_specs=VMEM,
        out_shape=shape(ways, PACKED, HEAD_DIM),
    )(query_states, key_states, value_states, saved_output, output_grad, normalizer.T)
    mine = lax.all_to_all(packed, KCOL, 0, 0)
    spread, qg = pl.pallas_call(
        spread_kernel,
        compiler_params=SMALL,
        in_specs=[VMEM],
        out_specs=[VMEM] * 2,
        out_shape=[shape(blocks, REACH, 2 * STRIP, HEAD_DIM), shape(ways, 2 * STRIP, HEAD_DIM)],
    )(mine)
    keys = lax.all_to_all(spread, "qrow", 0, 0)
    far = from_partner(qg, 2)
    others = [from_partner(qg, 1), far, from_partner(far, 1)]
    *dq_parts, dkv_part = call_tiles(place, doc_lengths, mine, qg, *others, keys)
    dkv = lax.all_to_all(dkv_part, "qrow", 0, 0)
    dq_parts = [dq_parts[0]] + [from_partner(dq_parts[s], s) for s in range(1, WAYS)]
    sums = pl.pallas_call(
        collect_kernel,
        compiler_params=SMALL,
        in_specs=[VMEM] * 5,
        out_specs=VMEM,
        out_shape=shape(ways, 3 * STRIP, HEAD_DIM),
    )(*dq_parts, dkv)
    back = lax.all_to_all(sums, KCOL, 0, 0)
    width = HEADS * HEAD_DIM
    return tuple(
        pl.pallas_call(
            unpack_kernel,
            compiler_params=SMALL,
            in_specs=[VMEM],
            out_specs=[VMEM] * 3,
            out_shape=[shape(CHUNK, width)] * 3,
        )(back)
    )


def solution(mesh):
    finer = Mesh(mesh.devices.reshape(mesh.shape["qrow"], HEADS, WAYS), ("qrow",) + KCOL)
    rows = P(("qrow",) + KCOL, None)
    keys = P(KCOL + ("qrow",), None)
    return jax.shard_map(
        per_device,
        mesh=finer,
        in_specs=(rows, keys, keys, rows, rows, rows, P()),
        out_specs=(rows, keys, keys),
        check_vma=False,
    )
```
